32 devices in a mesh: replica: 8 (over z, core), shard: 4 (over y, x).
Axes of the slice: x: 2, y: 2, z: 4, core: 2. Of those that a mesh axis runs over, the one named last changes fastest.
Arguments:
- tokens: bfloat16 [24576, 768], P(('replica', 'shard')), may hold values from -6 to 6
- cotangent: bfloat16 [24576, 768], P(('replica', 'shard')), may hold values from -6 to 6
- doc_lengths: int32 [32, 4], P(('replica', 'shard')), may hold values from 0 to 768, as said below
- in_weight: bfloat16 [768, 3352], P('shard'), may hold values from -0.21875 to 0.21875
- out_weight: bfloat16 [1536, 768], P('shard'), may hold values from -0.15625 to 0.15625
- conv_weight: bfloat16 [4, 1792], P(None, 'shard'), may hold values from -3 to 3
- conv_bias: bfloat16 [1792], P('shard'), may hold values from -3 to 3
- step_bias: bfloat16 [24], P('shard'), may hold values from -5 to -2
- decay_log: bfloat16 [24], P('shard'), may hold values from 0 to 2.796875
- skip_gain: bfloat16 [24], P('shard'), may hold values from 0.5 to 1.5
- norm_gain: bfloat16 [768], P('shard'), may hold values from 0.5 to 1.5
- gate_gain: bfloat16 [1536], P('shard'), may hold values from 0.5 to 1.5
Outputs:
- layer_out: float32 [24576, 768], P(('replica', 'shard'))
- input_grad: float32 [24576, 768], P(('replica', 'shard'))
- in_weight_grad: float32 [768, 3352], P('shard')
- out_weight_grad: float32 [1536, 768], P('shard')
- conv_weight_grad: float32 [4, 1792], P(None, 'shard')
- conv_bias_grad: float32 [1792], P('shard')
- step_bias_grad: float32 [24], P('shard')
- decay_log_grad: float32 [24], P('shard')
- skip_gain_grad: float32 [24], P('shard')
- norm_gain_grad: float32 [768], P('shard')
- gate_gain_grad: float32 [1536], P('shard')
The draws below stay inside these ranges and needn't reach their ends.
Inputs may be any that keep to these rules, and one draw needn't show every extreme that they name: `doc_lengths`: row k lists the lengths of the sequences packed in order from the start of device block k; a zero is an empty entry; every row sums to at most 768, and some row is one sequence of 768 slots.
All inputs are finite; a program needn't handle non-finite values.
Results may differ from the reference program's by a relative error of at most 0.0071.
Values may be sent and summed in bfloat16 or wider, within the bound.
A program may use at most 256 MiB of HBM per device.

```python
import jax
import jax.numpy as jnp
from jax import lax

D = 768
HEADS = 24
KERNEL = 4
BLOCK = 256
TOK_DEV = 768
SLOTS = 4
INNER = 1536
CONVD = 1792
PROJ = 3352
TOKENS = 24576
N_REPLICA = 8
N_SHARD = 4


def draw_doc_lengths(key, part):
    devices_all = N_REPLICA * N_SHARD
    subkeys = jax.random.split(jax.random.fold_in(key, 17), 3)
    fills = jax.random.randint(subkeys[0], (devices_all,), TOK_DEV // 4, TOK_DEV + 1).astype(jnp.int32)
    cuts = jnp.sort(jax.random.randint(subkeys[1], (devices_all, SLOTS - 1), 0, TOK_DEV + 1).astype(jnp.int32), axis=1)
    scaled = cuts * fills[:, None] // TOK_DEV
    bounds = jnp.concatenate([jnp.zeros((devices_all, 1), jnp.int32), scaled, fills[:, None]], axis=1)
    lengths = bounds[:, 1:] - bounds[:, :-1]
    chosen = jax.random.randint(subkeys[2], (), 0, devices_all).astype(jnp.int32)
    single = jnp.concatenate([jnp.full((1,), TOK_DEV, jnp.int32), jnp.zeros((SLOTS - 1,), jnp.int32)])
    rows_index = jnp.arange(devices_all, dtype=jnp.int32)
    lengths = jnp.where((rows_index == chosen)[:, None], single[None, :], lengths)
    return lengths.astype(jnp.int32)


def block_levels(stream_key, dims, cuts, least, high):
    gain = 1.0
    for dim, blocks in cuts:
        draws = jax.random.uniform(jax.random.fold_in(jax.random.fold_in(stream_key, 6), dim), (blocks,), jnp.float32, least / len(cuts), high / len(cuts))
        gain = gain * jnp.repeat(jnp.exp(draws), dims[dim] // blocks).reshape((-1,) + (1,) * (len(dims) - 1 - dim))
    return gain


def centred(stream_key, extent, width, bound, cuts=(), held_as=jnp.bfloat16):
    loudness = block_levels(stream_key, extent, cuts, -0.22, 0.18) if cuts else 1.0
    entries = jax.random.normal(stream_key, extent, jnp.float32) * width * loudness
    return jnp.minimum(jnp.maximum(entries, -bound), bound).astype(held_as)


def setup_inputs(seed: int = 0) -> dict:
    key_list = jax.random.split(jax.random.key(seed), 13)
    return {
        "tokens": centred(key_list[0], (TOKENS, D), 1.0, 6.0, ((0, 32),)),
        "cotangent": centred(key_list[1], (TOKENS, D), 1.0, 6.0, ((0, 32),)),
        "doc_lengths": draw_doc_lengths(jax.random.fold_in(key_list[12], 71), 0),
        "in_weight": centred(key_list[3], (D, PROJ), D ** -0.5, 0.21875, ((0, 4),)),
        "out_weight": centred(key_list[4], (INNER, D), INNER ** -0.5, 0.15625, ((0, 4),)),
        "conv_weight": centred(key_list[5], (KERNEL, CONVD), KERNEL ** -0.5, 3.0, ((1, 4),)),
        "conv_bias": centred(key_list[6], (CONVD,), 0.5, 3.0, ((0, 4),)),
        "step_bias": jnp.clip(-5.0 + 3.0 * jax.random.uniform(key_list[7], (HEADS,), jnp.float32) ** block_levels(key_list[7], (HEADS,), ((0, 4),), -0.2, 0.2), -5.0, -2.0).astype(jnp.bfloat16),
        "decay_log": jnp.clip(2.796875 * jax.random.uniform(key_list[8], (HEADS,), jnp.float32) ** block_levels(key_list[8], (HEADS,), ((0, 4),), -0.2, 0.2), 0.0, 2.796875).astype(jnp.bfloat16),
        "skip_gain": jnp.clip(0.5 + 1.0 * jax.random.uniform(key_list[9], (HEADS,), jnp.float32) ** block_levels(key_list[9], (HEADS,), ((0, 4),), -0.2, 0.2), 0.5, 1.5).astype(jnp.bfloat16),
        "norm_gain": jnp.clip(1.0 + 0.1 * jax.random.normal(key_list[10], (D,), jnp.float32), 0.5, 1.5).astype(jnp.bfloat16),
        "gate_gain": jnp.clip(1.0 + 0.1 * jax.random.normal(key_list[11], (INNER,), jnp.float32), 0.5, 1.5).astype(jnp.bfloat16),
    }


EPS = 1e-05
HIGH = lax.Precision.HIGHEST

def prenorm(values, gain_vec):
    scales = lax.rsqrt(lax.optimization_barrier(jnp.mean(values * values, axis=1, keepdims=True)) + EPS)
    return values * scales * gain_vec[None, :]

def segments_of(lengths, length):
    boundary = jnp.cumsum(lengths).astype(jnp.int32)
    places = jnp.arange(length, dtype=jnp.int32)
    segment = lax.optimization_barrier(jnp.sum((places[:, None] >= boundary[None, :]).astype(jnp.int32), axis=1)).astype(jnp.int32)
    return (segment, places < boundary[-1])

def conv_causal(values, segment, kernel_taps, bias_row):
    kernel_len = kernel_taps.shape[0]
    result = bias_row[None, :] + kernel_taps[kernel_len - 1][None, :] * values
    for offset in range(1, kernel_len):
        shifted = jnp.concatenate([jnp.zeros((offset, values.shape[1]), values.dtype), values[:-offset]], axis=0)
        earlier = jnp.concatenate([jnp.full((offset,), -1, jnp.int32), segment[:-offset]], axis=0)
        result = result + kernel_taps[kernel_len - 1 - offset][None, :] * jnp.where((earlier == segment)[:, None], shifted, 0.0)
    return result

def scan_blocks(inputs, spacing, decays, key_rows, query_rows, segment, block_len):
    length, head_count, head_width = inputs.shape
    block_count = length // block_len
    state_size = key_rows.shape[1]
    places = jnp.arange(block_len, dtype=jnp.int32)
    lower_tri = places[:, None] >= places[None, :]
    inputs_b = inputs.reshape(block_count, block_len, head_count, head_width)
    spacing_b = spacing.reshape(block_count, block_len, head_count)
    keys_b = key_rows.reshape(block_count, block_len, state_size)
    queries_b = query_rows.reshape(block_count, block_len, state_size)
    segment_b = segment.reshape(block_count, block_len)
    cumulated = jnp.cumsum(spacing_b * decays[None, None, :], axis=1)
    same_seg = (segment_b[:, :, None] == segment_b[:, None, :]) & lower_tri[None]
    by_head = jnp.swapaxes(cumulated, 1, 2)
    spread = by_head[:, :, :, None] - by_head[:, :, None, :]
    within = jnp.where(same_seg[:, None], jnp.exp(jnp.where(same_seg[:, None], spread, 0.0)), 0.0)
    gram_mat = jnp.einsum('bin,bjn->bij', queries_b, keys_b, precision=HIGH)
    mixing = within * gram_mat[:, None] * jnp.swapaxes(spacing_b, 1, 2)[:, :, None, :]
    inside = jnp.einsum('bhij,bjhp->bihp', mixing, inputs_b, precision=HIGH)
    final_seg = segment_b[:, block_len - 1]
    before = jnp.concatenate([jnp.full((1,), -1, jnp.int32), final_seg[:-1]], axis=0)
    end_decay = cumulated[:, block_len - 1]
    ending = jnp.where((segment_b == final_seg[:, None])[:, :, None], jnp.exp(end_decay[:, None, :] - cumulated), 0.0) * spacing_b
    retained = jnp.where((final_seg == before)[:, None], jnp.exp(end_decay), 0.0)
    injected = jnp.einsum('bjh,bjhp,bjn->bhpn', ending, inputs_b, keys_b, precision=HIGH)

    def advance(states, pieces):
        kept, added = pieces
        return (kept[:, None, None] * states + added, states)
    initial = jnp.zeros((head_count, head_width, state_size), jnp.float32)
    _, starts = lax.scan(advance, initial, (retained, injected))
    carry_rows = (segment_b == before[:, None]).astype(jnp.float32)[:, :, None] * jnp.exp(cumulated)
    incoming = jnp.einsum('bin,bhpn->bihp', queries_b, starts, precision=HIGH) * carry_rows[:, :, :, None]
    return (inside + incoming).reshape(length, head_count, head_width)

def mixer(projected, segment, kernel_taps, bias_row, step_shift, decay_logs, skip_row, gate_row):
    length = projected.shape[0]
    inner = gate_row.shape[0]
    head_count = step_shift.shape[0]
    channels = kernel_taps.shape[1]
    state_size = (channels - inner) // 2
    gate_rows = projected[:, :inner]
    conv_in = projected[:, inner:inner + channels]
    step_raw = projected[:, inner + channels:]
    conv_out = jax.nn.silu(conv_causal(conv_in, segment, kernel_taps, bias_row))
    inputs = conv_out[:, :inner].reshape(length, head_count, inner // head_count)
    key_rows = conv_out[:, inner:inner + state_size]
    query_rows = conv_out[:, inner + state_size:]
    spacing = jax.nn.softplus(step_raw + step_shift[None, :])
    decays = -jnp.exp(decay_logs)
    outputs = scan_blocks(inputs, spacing, decays, key_rows, query_rows, segment, BLOCK)
    outputs = outputs + skip_row[None, :, None] * inputs
    gated = outputs.reshape(length, inner) * jax.nn.silu(gate_rows)
    return prenorm(gated, gate_row)

def device_pass(tokens, cotangent, lengths, params):
    segment, valid = segments_of(lengths, tokens.shape[0])
    in_full, out_full = (params[0], params[1])
    smalls = tuple((piece.astype(jnp.float32) for piece in (params[2], params[3], params[4], params[5], params[6], params[8])))
    gain_vec = params[7].astype(jnp.float32)
    values = tokens.astype(jnp.float32)
    normed = prenorm(values, gain_vec).astype(jnp.bfloat16)
    projected = jnp.dot(normed, in_full, preferred_element_type=jnp.float32)

    def apply_mixer(proj_in, taps, bias_row, shift, logs, skip_row, gate_row):
        return mixer(proj_in, segment, taps, bias_row, shift, logs, skip_row, gate_row)
    mixed, mixer_back = jax.vjp(apply_mixer, projected, *smalls)
    mixed_b = mixed.astype(jnp.bfloat16)
    valid_col = valid.astype(jnp.float32)[:, None]
    layer = values + valid_col * jnp.dot(mixed_b, out_full, preferred_element_type=jnp.float32)
    masked = cotangent * valid.astype(jnp.bfloat16)[:, None]
    grad_outw = lax.dot_general(mixed_b, masked, (((0,), (0,)), ((), ())), preferred_element_type=jnp.float32)
    grad_mixed = lax.dot_general(masked, out_full, (((1,), (1,)), ((), ())), preferred_element_type=jnp.float32)
    mixer_grads = mixer_back(grad_mixed)
    grad_projected = mixer_grads[0]
    grad_proj = grad_projected.astype(jnp.bfloat16)
    grad_inw = lax.dot_general(normed, grad_proj, (((0,), (0,)), ((), ())), preferred_element_type=jnp.float32)
    grad_normed = lax.dot_general(grad_proj, in_full, (((1,), (1,)), ((), ())), preferred_element_type=jnp.float32)
    _, norm_back = jax.vjp(prenorm, values, gain_vec)
    grad_norm_in, grad_gain = norm_back(grad_normed)
    input_grad = cotangent.astype(jnp.float32) + grad_norm_in
    grads = (grad_inw, grad_outw, mixer_grads[1], mixer_grads[2], mixer_grads[3], mixer_grads[4], mixer_grads[5], grad_gain, mixer_grads[6])
    return (layer, input_grad, grads)

def reference(tokens, cotangent, doc_lengths, in_weight, out_weight, conv_weight, conv_bias, step_bias, decay_log, skip_gain, norm_gain, gate_gain):
    devices_all = N_REPLICA * N_SHARD
    params = (in_weight, out_weight, conv_weight, conv_bias, step_bias, decay_log, skip_gain, norm_gain, gate_gain)
    blocks_in = tokens.reshape(devices_all, TOK_DEV, D)
    blocks_cot = cotangent.reshape(devices_all, TOK_DEV, D)
    zeros_all = tuple((jnp.zeros(piece.shape, jnp.float32) for piece in params))

    def per_device(totals, pieces):
        layer, input_grad, grads = device_pass(pieces[0], pieces[1], pieces[2], params)
        return (tuple((first + second for first, second in zip(totals, grads))), (layer, input_grad))
    totals, (layers, inputs_grad) = lax.scan(per_device, zeros_all, (blocks_in, blocks_cot, doc_lengths))
    return (layers.reshape(TOKENS, D), inputs_grad.reshape(TOKENS, D), totals[0], totals[1], totals[2], totals[3], totals[4], totals[5], totals[6], totals[7], totals[8])
```

```python
import functools

import jax
import jax.numpy as jnp
from jax import lax
from jax.experimental import pallas as pl
from jax.experimental.pallas import tpu as pltpu
from jax.sharding import PartitionSpec as P

BLOCK = 256
LANES = 128
EPS = 1e-05
HIGH = lax.Precision.HIGHEST
BF = jnp.bfloat16
F32 = jnp.float32


def dot(a, b, dims=((1,), (0,)), precision=None):
    return lax.dot_general(a, b, (dims, ((), ())), preferred_element_type=F32, precision=precision)


def split(v):
    hi = v.astype(BF)
    return hi, (v - hi.astype(F32)).astype(BF)


def dot_split(mix_hi, mix_lo, v, dims):
    hi, lo = split(v)
    width = v.shape[1]
    both = dot(mix_hi, jnp.concatenate([hi, lo], axis=1), dims)
    return both[:, :width] + both[:, width:] + dot(mix_lo, hi, dims)


def prenorm(values, gain_vec):
    scales = lax.rsqrt(jnp.mean(values * values, axis=1, keepdims=True) + EPS)
    return values * scales * gain_vec[None, :]


def segments_of(lengths, length):
    boundary = jnp.cumsum(lengths)
    places = jnp.arange(length, dtype=jnp.int32)
    segment = jnp.sum((places[:, None] >= boundary[None, :]).astype(jnp.int32), axis=1)
    return (segment, places < boundary[-1])


def conv_causal(values, masks, kernel_taps, bias_row):
    kernel_len = kernel_taps.shape[0]
    result = bias_row[None, :] + kernel_taps[kernel_len - 1][None, :] * values
    for offset in range(1, kernel_len):
        shifted = jnp.concatenate(
            [jnp.zeros((offset, values.shape[1]), values.dtype), values[:-offset]], axis=0
        )
        result = result + kernel_taps[kernel_len - 1 - offset][None, :] * jnp.where(
            masks[offset - 1][:, None], shifted, 0.0
        )
    return result


def mixer_kernel(
    inner, taps_n, block, width,
    z_ref, cin_ref, gm_ref, gain_ref, taps_ref, bias_ref, skip_ref, mask_ref, gram_ref,
    rows_ref, cols_ref, fac_ref,
    dz_ref, dcin_ref, mixed_ref, dgram_ref, dc_ref, ddt_ref, sums_ref,
    pre_s, u_s, yd_s, yo_s, mix_s, low_s, ss_s, q_s,
):
    phase, g = pl.program_id(0), pl.program_id(1)
    length = z_ref.shape[0]
    nb = length // block
    heads = LANES // width

    def col(k, rows):
        parts = [
            jnp.broadcast_to(cols_ref[0, rows, k * heads + h : k * heads + h + 1], (block, width))
            for h in range(heads)
        ]
        return jnp.concatenate(parts, axis=1)

    def shifted_in(k):
        return pltpu.roll(cin_ref[...], k, 0) * mask_ref[k - 1]

    blocks = [slice(i * block, (i + 1) * block) for i in range(nb)]

    @pl.when((phase == 0) & (g == 0))
    def _():
        ss_s[...] = jnp.zeros_like(ss_s)
        q_s[...] = jnp.zeros_like(q_s)
        dgram_ref[...] = jnp.zeros_like(dgram_ref)
        dc_ref[...] = jnp.zeros_like(dc_ref)
        ddt_ref[...] = jnp.zeros_like(ddt_ref)

    @pl.when(phase == 0)
    def _():
        pre = bias_ref[0:1, :] + taps_ref[taps_n - 1 : taps_n, :] * cin_ref[...]
        for k in range(1, taps_n):
            pre = pre + taps_ref[taps_n - 1 - k : taps_n - k, :] * shifted_in(k)
        pre_s[g] = pre
        vs = []
        for i in range(nb):
            r = blocks[i]
            p_r = pre_s[g, r, :]
            x = p_r * jax.nn.sigmoid(p_r)
            u = x * col(1, r)
            u_s[g, r, :] = u
            vs.append((u * col(3, r)).astype(BF))
            ys = []
            for h in range(heads):
                spread = cols_ref[0, r, h : h + 1] - rows_ref[0, h : h + 1, r]
                hi, lo = split(jnp.exp(jnp.minimum(spread, 0.0)) * gram_ref[r, r])
                mix_s[g, h, i] = hi
                low_s[g, h, i] = lo
                ys.append(dot_split(hi, lo, u[:, h * width : (h + 1) * width], ((1,), (0,))))
            yd = jnp.concatenate(ys, axis=1)
            yd_s[g, r, :] = yd
            yo = jnp.zeros((block, LANES), F32)
            for j in range(i):
                yo = yo + dot(gram_ref[r, blocks[j]].astype(BF), vs[j]) * fac_ref[i * nb + j : i * nb + j + 1, :]
            yo_s[g, r, :] = yo
            z = z_ref[r, :]
            gated = (yd + yo * col(2, r) + skip_ref[0:1, :] * x) * (z * jax.nn.sigmoid(z))
            ss_s[r, :] += gated * gated
            q_s[r, :] += gm_ref[r, :] * gain_ref[0:1, :] * gated

    @pl.when((phase == 1) & (g == 0))
    def _():
        scale = lax.rsqrt(jnp.sum(ss_s[...], axis=1, keepdims=True) / inner + EPS)
        coef = jnp.sum(q_s[...], axis=1, keepdims=True) * scale * scale * scale / inner
        ss_s[...] = jnp.broadcast_to(scale, ss_s.shape)
        q_s[...] = jnp.broadcast_to(coef, q_s.shape)

    @pl.when(phase == 1)
    def _():
        lane = lax.broadcasted_iota(jnp.int32, (LANES, LANES), 0) // width
        target = lax.broadcasted_iota(jnp.int32, (LANES, LANES), 1)
        pick = jnp.where(lane + g * heads == target, 1.0, 0.0).astype(BF)

        def by_head(d):
            hi = d.astype(BF)
            lo = (d - hi.astype(F32)).astype(BF)
            return dot(hi, pick) + dot(lo, pick)

        dys_all, ws, vs = [], [], []
        dskip = jnp.zeros((1, LANES), F32)
        dgain = jnp.zeros((1, LANES), F32)
        for i in range(nb):
            r = blocks[i]
            p_r = pre_s[g, r, :]
            x = p_r * jax.nn.sigmoid(p_r)
            z = z_ref[r, :]
            sig = jax.nn.sigmoid(z)
            act = z * sig
            a = col(2, r)
            y = yd_s[g, r, :] + yo_s[g, r, :] * a + skip_ref[0:1, :] * x
            gated = y * act
            scale = ss_s[r, :]
            mixed_ref[r, :] = (gated * scale * gain_ref[0:1, :]).astype(BF)
            gm = gm_ref[r, :]
            dgain = dgain + jnp.sum(gm * gated * scale, axis=0, keepdims=True)
            dgated = gm * gain_ref[0:1, :] * scale - gated * q_s[r, :]
            dz_ref[r, :] = (dgated * y * (sig + act * (1.0 - sig))).astype(BF)
            dy = dgated * act
            dskip = dskip + jnp.sum(dy * x, axis=0, keepdims=True)
            dys_all.append(dy)
            ws.append((dy * a).astype(BF))
            vs.append((u_s[g, r, :] * col(3, r)).astype(BF))
        for j in range(nb):
            r = blocks[j]
            dy = dys_all[j]
            dyb = dy.astype(BF)
            u = u_s[g, r, :]
            ub = u.astype(BF)
            dus = []
            dgram = jnp.zeros((block, block), F32)
            for h in range(heads):
                lanes = slice(h * width, (h + 1) * width)
                dus.append(dot_split(mix_s[g, h, j], low_s[g, h, j], dy[:, lanes], ((0,), (0,))))
                spread = cols_ref[0, r, h : h + 1] - rows_ref[0, h : h + 1, r]
                decay = jnp.exp(jnp.minimum(spread, 0.0))
                dgram = dgram + decay * dot(dyb[:, lanes], ub[:, lanes], ((1,), (1,)))
            dgram_ref[r, r] += dgram
            du = jnp.concatenate(dus, axis=1)
            dv = jnp.zeros((block, LANES), F32)
            for i in range(j + 1, nb):
                fac = fac_ref[i * nb + j : i * nb + j + 1, :]
                dv = dv + dot(gram_ref[blocks[i], r].astype(BF), ws[i], ((0,), (0,))) * fac
                dgram_ref[blocks[i], r] += dot(
                    (ws[i].astype(F32) * fac).astype(BF), vs[j], ((1,), (1,))
                )
            dc_ref[r, :] += by_head(
                dy * yd_s[g, r, :]
                + ws[j].astype(F32) * yo_s[g, r, :]
                - u * du
                - vs[j].astype(F32) * dv
            )
            du = du + dv * col(3, r)
            p_r = pre_s[g, r, :]
            sig = jax.nn.sigmoid(p_r)
            x = p_r * sig
            ddt_ref[r, :] += by_head(du * x)
            dx = skip_ref[0:1, :] * dy + du * col(1, r)
            yd_s[g, r, :] = dx * (sig + x * (1.0 - sig))
        dpre = yd_s[g]
        dcin = taps_ref[taps_n - 1 : taps_n, :] * dpre
        sums_ref[taps_n - 1 : taps_n, :] = jnp.sum(dpre * cin_ref[...], axis=0, keepdims=True)
        for k in range(1, taps_n):
            masked = dpre * mask_ref[k - 1]
            dcin = dcin + taps_ref[taps_n - 1 - k : taps_n - k, :] * pltpu.roll(masked, length - k, 0)
            sums_ref[taps_n - 1 - k : taps_n - k, :] = jnp.sum(
                masked * pltpu.roll(cin_ref[...], k, 0), axis=0, keepdims=True
            )
        dcin_ref[...] = dcin.astype(BF)
        sums_ref[taps_n : taps_n + 1, :] = jnp.sum(dpre, axis=0, keepdims=True)
        sums_ref[taps_n + 1 : taps_n + 2, :] = dskip
        sums_ref[taps_n + 2 : taps_n + 3, :] = dgain


def mixer_call(projected, gm, gain, taps, bias, skip, conv_masks, gram, spacing, cum, heads_all):
    length = projected.shape[0]
    inner = gain.shape[0]
    taps_n = taps.shape[0]
    width = inner // heads_all
    heads = LANES // width
    groups = inner // LANES
    block = BLOCK
    nb = length // block
    ends = cum[block - 1 :: block]
    starts = jnp.concatenate([jnp.zeros((1, heads_all), F32), ends[:-1]], axis=0)
    cum_b = cum.reshape(nb, block, heads_all)
    enter = jnp.exp(cum_b - starts[:, None]).reshape(length, heads_all)
    leave = jnp.exp(ends[:, None] - cum_b).reshape(length, heads_all)
    fac = jnp.exp(jnp.minimum(starts[:, None] - ends[None, :], 0.0)).reshape(nb * nb, heads_all)
    fac = jnp.repeat(fac, width, axis=1)
    cols = jnp.stack([cum, spacing, enter, leave], axis=1).reshape(length, 4, groups, heads)
    cols = cols.transpose(2, 0, 1, 3).reshape(groups, length, 4 * heads)
    rows = cum.T.reshape(groups, heads, length)
    wide = lambda m: jnp.broadcast_to(m[:, None], (length, LANES)).astype(F32)
    masks = jnp.stack([wide(m) for m in conv_masks])
    n_sum = taps_n + 3

    part = lambda off: pl.BlockSpec((length, LANES), lambda p, g: (0, off + g))
    row = lambda n: pl.BlockSpec((n, LANES), lambda p, g: (0, g))
    full = lambda *s: pl.BlockSpec(s, lambda p, g: (0,) * len(s))
    late = lambda n: pl.BlockSpec((n, LANES), lambda p, g: (0, p * g))
    sds = jax.ShapeDtypeStruct
    return pl.pallas_call(
        functools.partial(mixer_kernel, inner, taps_n, block, width),
        grid=(2, groups),
        in_specs=[
            part(0), part(groups), part(0), row(1), row(taps_n), row(1), row(1),
            full(taps_n - 1, length, LANES), full(length, length),
            pl.BlockSpec((1, heads, length), lambda p, g: (g, 0, 0)),
            pl.BlockSpec((1, length, 4 * heads), lambda p, g: (g, 0, 0)),
            row(nb * nb),
        ],
        out_specs=[
            late(length), late(length), late(length), full(length, length),
            full(length, LANES), full(length, LANES), late(n_sum),
        ],
        out_shape=[
            sds((length, inner), BF), sds((length, inner), BF), sds((length, inner), BF),
            sds((length, length), F32), sds((length, LANES), F32), sds((length, LANES), F32),
            sds((n_sum, inner), F32),
        ],
        scratch_shapes=[
            pltpu.VMEM((groups, length, LANES), F32),
            pltpu.VMEM((groups, length, LANES), F32),
            pltpu.VMEM((groups, length, LANES), F32),
            pltpu.VMEM((groups, length, LANES), F32),
            pltpu.VMEM((groups, heads, nb, block, block), BF),
            pltpu.VMEM((groups, heads, nb, block, block), BF),
            pltpu.VMEM((length, LANES), F32),
            pltpu.VMEM((length, LANES), F32),
        ],
        compiler_params=pltpu.CompilerParams(
            vmem_limit_bytes=60 * 1024 * 1024, dimension_semantics=("arbitrary", "arbitrary")
        ),
        cost_estimate=pl.CostEstimate(
            flops=20 * length * block * inner, bytes_accessed=40 * length * inner, transcendentals=0
        ),
    )(
        projected, projected, gm, gain[None], taps[:, :inner], bias[None, :inner],
        jnp.repeat(skip, width)[None], masks, gram, rows, cols, fac,
    )


def device_part(tokens, cotangent, lengths, in_full, out_full, smalls, gain_vec):
    length = tokens.shape[0]
    segment, valid = segments_of(lengths, length)
    taps, bias, step_bias, decay_log, skip, gate_gain = smalls
    inner = gate_gain.shape[0]
    channels = taps.shape[1]
    heads_all = step_bias.shape[0]
    state = (channels - inner) // 2
    values = tokens.astype(F32)
    normed = prenorm(values, gain_vec).astype(BF)
    projected = dot(normed, in_full)
    masked = cotangent * valid.astype(BF)[:, None]
    grad_mixed = dot(masked, out_full, ((1,), (1,)))
    places = jnp.arange(length, dtype=jnp.int32)
    lower = places[:, None] >= places[None, :]
    conv_masks = [
        (places >= k) & (jnp.roll(segment, k) == segment) for k in range(1, taps.shape[0])
    ]
    same = lower & (segment[:, None] == segment[None, :])

    def gram_of(cin, taps_bc, bias_bc):
        out = jax.nn.silu(conv_causal(cin, conv_masks, taps_bc, bias_bc))
        return jnp.where(same, dot(out[:, state:], out[:, :state], ((1,), (1,)), HIGH), 0.0)

    def steps_of(raw, shift, logs):
        spacing = jax.nn.softplus(raw + shift[None, :])
        cum = dot(lower.astype(F32), spacing * -jnp.exp(logs)[None, :], precision=HIGH)
        return spacing, cum

    gram, gram_back = jax.vjp(
        gram_of, projected[:, 2 * inner : inner + channels], taps[:, inner:], bias[inner:]
    )
    (spacing, cum), steps_back = jax.vjp(
        steps_of, projected[:, inner + channels :], step_bias, decay_log
    )
    dz, dcin, mixed, dgram, dcum, dspacing, sums = mixer_call(
        projected, grad_mixed, gate_gain, taps, bias, skip, conv_masks, gram, spacing, cum, heads_all
    )
    d_bc, dtaps_bc, dbias_bc = gram_back(dgram)
    d_raw, d_shift, d_logs = steps_back((dspacing[:, :heads_all], dcum[:, :heads_all]))
    n = taps.shape[0]
    d_taps = jnp.concatenate([sums[:n], dtaps_bc], axis=1)
    d_bias = jnp.concatenate([sums[n], dbias_bc])
    d_skip = jnp.sum(sums[n + 1].reshape(heads_all, -1), axis=1)
    d_gate_gain = sums[n + 2]
    grad_proj = jnp.concatenate([dz, dcin, d_bc.astype(BF), d_raw.astype(BF)], axis=1)
    layer = values + valid.astype(F32)[:, None] * dot(mixed, out_full)
    grad_outw = dot(mixed, masked, ((0,), (0,)))
    grad_inw = dot(normed, grad_proj, ((0,), (0,)))
    grad_normed = dot(grad_proj, in_full, ((1,), (1,)))
    _, norm_back = jax.vjp(prenorm, values, gain_vec)
    grad_norm_in, grad_gain = norm_back(grad_normed)
    input_grad = cotangent.astype(F32) + grad_norm_in
    return layer, input_grad, (
        grad_inw, grad_outw, d_taps, d_bias, d_shift, d_logs, d_skip, grad_gain, d_gate_gain
    )


def moved(x, step):
    n_rep, n = lax.axis_size("replica"), lax.axis_size("shard")
    perm = []
    for r in range(n_rep):
        for s in range(n):
            to_r, to_s = step(r, s)
            perm.append((r * n + s, to_r * n + to_s))
    return lax.ppermute(x, ("replica", "shard"), perm)


def pick(x, i):
    return lax.dynamic_index_in_dim(x, i, 0, keepdims=False)


def ring_all(x, index, n, step):
    got = jnp.stack([x] + [moved(x, functools.partial(step, k)) for k in range(1, n)])
    return jnp.stack([pick(got, lax.rem(index - j + n, n)) for j in range(n)])


def ring_sum(parts, index, n, step):
    total = pick(parts, index).astype(F32)
    for k in range(1, n):
        total = total + moved(pick(parts, lax.rem(index + k, n)), functools.partial(step, k))
    return total


def shard_step(k, r, s):
    return r, (s + k) % lax.axis_size("shard")


def chip_step(k, r, s):
    return (r + 2 * k) % lax.axis_size("replica"), s


def core_step(r, s):
    return r ^ 1, s


def both_halves(mine, core, axis):
    other = moved(mine, core_step)
    first = jnp.where(core == 0, mine, other)
    second = jnp.where(core == 0, other, mine)
    return jnp.stack([first, second], axis=axis)


def gather_weight(shard, core, me, n):
    half = pick(shard.reshape(2, -1, shard.shape[1]), core)
    mine = ring_all(half, me, n, shard_step)
    return both_halves(mine, core, 1).reshape(-1, shard.shape[1])


def reduce_grad(grad, core, me, n, chip, chips, kind):
    columns = grad.shape[1]
    blocks = grad.astype(kind).reshape(n, 2, -1, columns)
    keep = lax.dynamic_index_in_dim(blocks, core, 1, keepdims=False)
    send = lax.dynamic_index_in_dim(blocks, 1 - core, 1, keepdims=False)
    pair = (keep.astype(F32) + moved(send, core_step).astype(F32)).astype(kind)
    mine = ring_sum(pair, me, n, shard_step).astype(kind)
    piece = ring_sum(mine.reshape(chips, -1, columns), chip, chips, chip_step).astype(kind)
    half = ring_all(piece, chip, chips, chip_step).reshape(-1, columns)
    return both_halves(half, core, 0).reshape(-1, columns).astype(F32)


def on_device(tokens, cotangent, doc_lengths, *shards):
    n, chips = lax.axis_size("shard"), lax.axis_size("replica") // 2
    me, rep = lax.axis_index("shard"), lax.axis_index("replica")
    core, chip = lax.rem(rep, 2), lax.div(rep, 2)
    small = jnp.concatenate([piece.reshape(-1) for piece in shards[2:]])
    small_all = ring_all(small, me, n, shard_step)
    out_full = gather_weight(shards[1], core, me, n)
    in_full = gather_weight(shards[0], core, me, n)
    smalls, at = [], 0
    for piece in shards[2:]:
        got = small_all[:, at : at + piece.size].astype(F32)
        at += piece.size
        if piece.ndim == 2:
            got = got.reshape(n, *piece.shape).transpose(1, 0, 2).reshape(piece.shape[0], -1)
        else:
            got = got.reshape(-1)
        smalls.append(got)
    gain_vec = smalls[5]
    layer, input_grad, grads = device_part(
        tokens, cotangent, doc_lengths[0], in_full, out_full, (*smalls[:5], smalls[6]), gain_vec
    )
    rows = []
    for piece, grad in zip(shards[2:], grads[2:]):
        if piece.ndim == 2:
            grad = grad.reshape(piece.shape[0], n, -1).transpose(1, 0, 2)
        rows.append(grad.reshape(n, -1))
    packed = jnp.concatenate(rows, axis=1)
    unit = 2 * chips * 8 * LANES
    packed = jnp.pad(packed, ((0, 0), (0, -packed.shape[1] % unit))).reshape(-1, LANES)
    reduce = functools.partial(reduce_grad, core=core, me=me, n=n, chip=chip, chips=chips)
    big_out = reduce(grads[1], kind=BF)
    big_in = reduce(grads[0], kind=BF)
    mine = reduce(packed, kind=F32).reshape(-1)
    outs, at = [], 0
    for piece in shards[2:]:
        outs.append(mine[at : at + piece.size].reshape(piece.shape))
        at += piece.size
    return (layer, input_grad, big_in, big_out, *outs)


def solution(mesh):
    tok = P(("replica", "shard"), None)
    weights = (P("shard", None), P("shard", None), P(None, "shard")) + (P("shard"),) * 6
    return jax.shard_map(
        on_device,
        mesh=mesh,
        in_specs=(tok, tok, tok) + weights,
        out_specs=(tok, tok) + weights,
        check_vma=False,
    )
```

```python
import functools

import jax
import jax.numpy as jnp
from jax import lax
from jax.experimental import pallas as pl
from jax.experimental.pallas import tpu as pltpu
from jax.sharding import PartitionSpec as P

BLOCK = 256
LANES = 128
EPS = 1e-05
HIGH = lax.Precision.HIGHEST
BF = jnp.bfloat16
F32 = jnp.float32


def dot(a, b, dims=((1,), (0,)), precision=None):
    return lax.dot_general(a, b, (dims, ((), ())), preferred_element_type=F32, precision=precision)


def split(v):
    hi = v.astype(BF)
    return hi, (v - hi.astype(F32)).astype(BF)


def dot_split(mix_hi, mix_lo, v, dims):
    hi, lo = split(v)
    width = v.shape[1]
    both = dot(mix_hi, jnp.concatenate([hi, lo], axis=1), dims)
    return both[:, :width] + both[:, width:] + dot(mix_lo, hi, dims)


def prenorm(values, gain_vec):
    scales = lax.rsqrt(jnp.mean(values * values, axis=1, keepdims=True) + EPS)
    return values * scales * gain_vec[None, :]


def segments_of(lengths, length):
    boundary = jnp.cumsum(lengths)
    places = jnp.arange(length, dtype=jnp.int32)
    segment = jnp.sum((places[:, None] >= boundary[None, :]).astype(jnp.int32), axis=1)
    return (segment, places < boundary[-1])


def conv_causal(values, masks, kernel_taps, bias_row):
    kernel_len = kernel_taps.shape[0]
    result = bias_row[None, :] + kernel_taps[kernel_len - 1][None, :] * values
    for offset in range(1, kernel_len):
        shifted = jnp.concatenate(
            [jnp.zeros((offset, values.shape[1]), values.dtype), values[:-offset]], axis=0
        )
        result = result + kernel_taps[kernel_len - 1 - offset][None, :] * jnp.where(
            masks[offset - 1][:, None], shifted, 0.0
        )
    return result


def mixer_kernel(
    inner, taps_n, block, width,
    z_ref, cin_ref, gm_ref, gain_ref, taps_ref, bias_ref, skip_ref, mask_ref, gram_ref,
    rows_ref, cols_ref, fac_ref,
    dz_ref, dcin_ref, mixed_ref, dgram_ref, dc_ref, ddt_ref, sums_ref,
    pre_s, u_s, yd_s, yo_s, mix_s, low_s, ss_s, q_s, gt_s,
):
    phase, g = pl.program_id(0), pl.program_id(1)
    length = z_ref.shape[0]
    nb = length // block
    heads = LANES // width

    def col(k, rows):
        parts = [
            jnp.broadcast_to(cols_ref[0, rows, k * heads + h : k * heads + h + 1], (block, width))
            for h in range(heads)
        ]
        return jnp.concatenate(parts, axis=1)

    def shifted_in(k):
        return pltpu.roll(cin_ref[...], k, 0) * mask_ref[k - 1]

    blocks = [slice(i * block, (i + 1) * block) for i in range(nb)]

    @pl.when((phase == 0) & (g == 0))
    def _():
        ss_s[...] = jnp.zeros_like(ss_s)
        q_s[...] = jnp.zeros_like(q_s)
        gt_s[...] = gram_ref[...].T.astype(BF)
        dgram_ref[...] = jnp.zeros_like(dgram_ref)
        dc_ref[...] = jnp.zeros_like(dc_ref)
        ddt_ref[...] = jnp.zeros_like(ddt_ref)

    @pl.when(phase == 0)
    def _():
        pre = bias_ref[0:1, :] + taps_ref[taps_n - 1 : taps_n, :] * cin_ref[...]
        for k in range(1, taps_n):
            pre = pre + taps_ref[taps_n - 1 - k : taps_n - k, :] * shifted_in(k)
        pre_s[g] = pre
        vs = []
        for i in range(nb):
            r = blocks[i]
            p_r = pre_s[g, r, :]
            x = p_r * jax.nn.sigmoid(p_r)
            u = x * col(1, r)
            u_s[g, r, :] = u
            vs.append((u * col(3, r)).astype(BF))
            ys = []
            for h in range(heads):
                spread = cols_ref[0, r, h : h + 1] - rows_ref[0, h : h + 1, r]
                hi, lo = split(jnp.exp(jnp.minimum(spread, 0.0)) * gram_ref[r, r])
                mix_s[g, h, i] = hi
                low_s[g, h, i] = lo
                ys.append(dot_split(hi, lo, u[:, h * width : (h + 1) * width], ((1,), (0,))))
            yd = jnp.concatenate(ys, axis=1)
            yd_s[g, r, :] = yd
            yo = jnp.zeros((block, LANES), F32)
            for j in range(i):
                yo = yo + dot(gram_ref[r, blocks[j]].astype(BF), vs[j]) * fac_ref[i * nb + j : i * nb + j + 1, :]
            yo_s[g, r, :] = yo
            z = z_ref[r, :]
            gated = (yd + yo * col(2, r) + skip_ref[0:1, :] * x) * (z * jax.nn.sigmoid(z))
            ss_s[r, :] += gated * gated
            q_s[r, :] += gm_ref[r, :] * gain_ref[0:1, :] * gated

    @pl.when((phase == 1) & (g == 0))
    def _():
        scale = lax.rsqrt(jnp.sum(ss_s[...], axis=1, keepdims=True) / inner + EPS)
        coef = jnp.sum(q_s[...], axis=1, keepdims=True) * scale * scale * scale / inner
        ss_s[...] = jnp.broadcast_to(scale, ss_s.shape)
        q_s[...] = jnp.broadcast_to(coef, q_s.shape)

    @pl.when(phase == 1)
    def _():
        lane = lax.broadcasted_iota(jnp.int32, (LANES, LANES), 0) // width
        target = lax.broadcasted_iota(jnp.int32, (LANES, LANES), 1)
        pick = jnp.where(lane + g * heads == target, 1.0, 0.0).astype(BF)

        def by_head(d):
            hi = d.astype(BF)
            lo = (d - hi.astype(F32)).astype(BF)
            return dot(hi, pick) + dot(lo, pick)

        dys_all, ws, vs = [], [], []
        dskip = jnp.zeros((1, LANES), F32)
        dgain = jnp.zeros((1, LANES), F32)
        for i in range(nb):
            r = blocks[i]
            p_r = pre_s[g, r, :]
            x = p_r * jax.nn.sigmoid(p_r)
            z = z_ref[r, :]
            sig = jax.nn.sigmoid(z)
            act = z * sig
            a = col(2, r)
            y = yd_s[g, r, :] + yo_s[g, r, :] * a + skip_ref[0:1, :] * x
            gated = y * act
            scale = ss_s[r, :]
            mixed_ref[r, :] = (gated * scale * gain_ref[0:1, :]).astype(BF)
            gm = gm_ref[r, :]
            dgain = dgain + jnp.sum(gm * gated * scale, axis=0, keepdims=True)
            dgated = gm * gain_ref[0:1, :] * scale - gated * q_s[r, :]
            dz_ref[r, :] = (dgated * y * (sig + act * (1.0 - sig))).astype(BF)
            dy = dgated * act
            dskip = dskip + jnp.sum(dy * x, axis=0, keepdims=True)
            dys_all.append(dy)
            ws.append((dy * a).astype(BF))
            vs.append((u_s[g, r, :] * col(3, r)).astype(BF))
        for j in range(nb):
            r = blocks[j]
            dy = dys_all[j]
            dyb = dy.astype(BF)
            u = u_s[g, r, :]
            ub = u.astype(BF)
            dy_t = dy.T
            dus = []
            dgram = jnp.zeros((block, block), F32)
            for h in range(heads):
                lanes = slice(h * width, (h + 1) * width)
                dys = dy_t[h * width : (h + 1) * width]
                d_hi, d_lo = split(dys)
                both = dot(jnp.concatenate([d_hi, d_lo], axis=0), mix_s[g, h, j])
                dus.append(both[:width] + both[width:] + dot(d_hi, low_s[g, h, j]))
                spread = cols_ref[0, r, h : h + 1] - rows_ref[0, h : h + 1, r]
                decay = jnp.exp(jnp.minimum(spread, 0.0))
                dgram = dgram + decay * dot(dyb[:, lanes], ub[:, lanes], ((1,), (1,)))
            dgram_ref[r, r] += dgram
            du = jnp.concatenate(dus, axis=0).T
            dv = jnp.zeros((block, LANES), F32)
            for i in range(j + 1, nb):
                fac = fac_ref[i * nb + j : i * nb + j + 1, :]
                dv = dv + dot(gt_s[r, blocks[i]], ws[i]) * fac
                dgram_ref[blocks[i], r] += dot(
                    (ws[i].astype(F32) * fac).astype(BF), vs[j], ((1,), (1,))
                )
            dc_ref[r, :] += by_head(
                dy * yd_s[g, r, :]
                + ws[j].astype(F32) * yo_s[g, r, :]
                - u * du
                - vs[j].astype(F32) * dv
            )
            du = du + dv * col(3, r)
            p_r = pre_s[g, r, :]
            sig = jax.nn.sigmoid(p_r)
            x = p_r * sig
            ddt_ref[r, :] += by_head(du * x)
            dx = skip_ref[0:1, :] * dy + du * col(1, r)
            yd_s[g, r, :] = dx * (sig + x * (1.0 - sig))
        dpre = yd_s[g]
        dcin = taps_ref[taps_n - 1 : taps_n, :] * dpre
        sums_ref[taps_n - 1 : taps_n, :] = jnp.sum(dpre * cin_ref[...], axis=0, keepdims=True)
        for k in range(1, taps_n):
            masked = dpre * mask_ref[k - 1]
            dcin = dcin + taps_ref[taps_n - 1 - k : taps_n - k, :] * pltpu.roll(masked, length - k, 0)
            sums_ref[taps_n - 1 - k : taps_n - k, :] = jnp.sum(
                masked * pltpu.roll(cin_ref[...], k, 0), axis=0, keepdims=True
            )
        dcin_ref[...] = dcin.astype(BF)
        sums_ref[taps_n : taps_n + 1, :] = jnp.sum(dpre, axis=0, keepdims=True)
        sums_ref[taps_n + 1 : taps_n + 2, :] = dskip
        sums_ref[taps_n + 2 : taps_n + 3, :] = dgain


def mixer_call(projected, gm, gain, taps, bias, skip, conv_masks, gram, spacing, cum, heads_all):
    length = projected.shape[0]
    inner = gain.shape[0]
    taps_n = taps.shape[0]
    width = inner // heads_all
    heads = LANES // width
    groups = inner // LANES
    block = BLOCK
    nb = length // block
    ends = cum[block - 1 :: block]
    starts = jnp.concatenate([jnp.zeros((1, heads_all), F32), ends[:-1]], axis=0)
    cum_b = cum.reshape(nb, block, heads_all)
    enter = jnp.exp(cum_b - starts[:, None]).reshape(length, heads_all)
    leave = jnp.exp(ends[:, None] - cum_b).reshape(length, heads_all)
    fac = jnp.exp(jnp.minimum(starts[:, None] - ends[None, :], 0.0)).reshape(nb * nb, heads_all)
    fac = jnp.repeat(fac, width, axis=1)
    cols = jnp.stack([cum, spacing, enter, leave], axis=1).reshape(length, 4, groups, heads)
    cols = cols.transpose(2, 0, 1, 3).reshape(groups, length, 4 * heads)
    rows = cum.T.reshape(groups, heads, length)
    wide = lambda m: jnp.broadcast_to(m[:, None], (length, LANES)).astype(F32)
    masks = jnp.stack([wide(m) for m in conv_masks])
    n_sum = taps_n + 3

    part = lambda off: pl.BlockSpec((length, LANES), lambda p, g: (0, off + g))
    row = lambda n: pl.BlockSpec((n, LANES), lambda p, g: (0, g))
    full = lambda *s: pl.BlockSpec(s, lambda p, g: (0,) * len(s))
    late = lambda n: pl.BlockSpec((n, LANES), lambda p, g: (0, p * g))
    sds = jax.ShapeDtypeStruct
    return pl.pallas_call(
        functools.partial(mixer_kernel, inner, taps_n, block, width),
        grid=(2, groups),
        in_specs=[
            part(0), part(groups), part(0), row(1), row(taps_n), row(1), row(1),
            full(taps_n - 1, length, LANES), full(length, length),
            pl.BlockSpec((1, heads, length), lambda p, g: (g, 0, 0)),
            pl.BlockSpec((1, length, 4 * heads), lambda p, g: (g, 0, 0)),
            row(nb * nb),
        ],
        out_specs=[
            late(length), late(length), late(length), full(length, length),
            full(length, LANES), full(length, LANES), late(n_sum),
        ],
        out_shape=[
            sds((length, inner), BF), sds((length, inner), BF), sds((length, inner), BF),
            sds((length, length), F32), sds((length, LANES), F32), sds((length, LANES), F32),
            sds((n_sum, inner), F32),
        ],
        scratch_shapes=[
            pltpu.VMEM((groups, length, LANES), F32),
            pltpu.VMEM((groups, length, LANES), F32),
            pltpu.VMEM((groups, length, LANES), F32),
            pltpu.VMEM((groups, length, LANES), F32),
            pltpu.VMEM((groups, heads, nb, block, block), BF),
            pltpu.VMEM((groups, heads, nb, block, block), BF),
            pltpu.VMEM((length, LANES), F32),
            pltpu.VMEM((length, LANES), F32),
            pltpu.VMEM((length, length), BF),
        ],
        compiler_params=pltpu.CompilerParams(
            vmem_limit_bytes=60 * 1024 * 1024, dimension_semantics=("arbitrary", "arbitrary")
        ),
        cost_estimate=pl.CostEstimate(
            flops=20 * length * block * inner, bytes_accessed=40 * length * inner, transcendentals=0
        ),
    )(
        projected, projected, gm, gain[None], taps[:, :inner], bias[None, :inner],
        jnp.repeat(skip, width)[None], masks, gram, rows, cols, fac,
    )


def device_part(tokens, cotangent, lengths, in_full, out_full, smalls, gain_vec):
    length = tokens.shape[0]
    segment, valid = segments_of(lengths, length)
    taps, bias, step_bias, decay_log, skip, gate_gain = smalls
    inner = gate_gain.shape[0]
    channels = taps.shape[1]
    heads_all = step_bias.shape[0]
    state = (channels - inner) // 2
    values = tokens.astype(F32)
    normed = prenorm(values, gain_vec).astype(BF)
    projected = dot(normed, in_full)
    masked = cotangent * valid.astype(BF)[:, None]
    grad_mixed = dot(masked, out_full, ((1,), (1,)))
    places = jnp.arange(length, dtype=jnp.int32)
    lower = places[:, None] >= places[None, :]
    conv_masks = [
        (places >= k) & (jnp.roll(segment, k) == segment) for k in range(1, taps.shape[0])
    ]
    same = lower & (segment[:, None] == segment[None, :])

    def gram_of(cin, taps_bc, bias_bc):
        out = jax.nn.silu(conv_causal(cin, conv_masks, taps_bc, bias_bc))
        return jnp.where(same, dot(out[:, state:], out[:, :state], ((1,), (1,)), HIGH), 0.0)

    def steps_of(raw, shift, logs):
        spacing = jax.nn.softplus(raw + shift[None, :])
        cum = dot(lower.astype(F32), spacing * -jnp.exp(logs)[None, :], precision=HIGH)
        return spacing, cum

    gram, gram_back = jax.vjp(
        gram_of, projected[:, 2 * inner : inner + channels], taps[:, inner:], bias[inner:]
    )
    (spacing, cum), steps_back = jax.vjp(
        steps_of, projected[:, inner + channels :], step_bias, decay_log
    )
    dz, dcin, mixed, dgram, dcum, dspacing, sums = mixer_call(
        projected, grad_mixed, gate_gain, taps, bias, skip, conv_masks, gram, spacing, cum, heads_all
    )
    grad_outw = dot(mixed, masked, ((0,), (0,)))
    grad_outw, dgram, dcum, dspacing, dz, dcin = lax.optimization_barrier(
        (grad_outw.astype(BF), dgram, dcum, dspacing, dz, dcin)
    )
    d_bc, dtaps_bc, dbias_bc = gram_back(dgram)
    d_raw, d_shift, d_logs = steps_back((dspacing[:, :heads_all], dcum[:, :heads_all]))
    n = taps.shape[0]
    d_taps = jnp.concatenate([sums[:n], dtaps_bc], axis=1)
    d_bias = jnp.concatenate([sums[n], dbias_bc])
    d_skip = jnp.sum(sums[n + 1].reshape(heads_all, -1), axis=1)
    d_gate_gain = sums[n + 2]
    grad_proj = jnp.concatenate([dz, dcin, d_bc.astype(BF), d_raw.astype(BF)], axis=1)
    grad_inw = dot(normed, grad_proj, ((0,), (0,)))
    grad_inw, mixed, grad_proj = lax.optimization_barrier((grad_inw.astype(BF), mixed, grad_proj))
    layer = values + valid.astype(F32)[:, None] * dot(mixed, out_full)
    grad_normed = dot(grad_proj, in_full, ((1,), (1,)))
    _, norm_back = jax.vjp(prenorm, values, gain_vec)
    grad_norm_in, grad_gain = norm_back(grad_normed)
    input_grad = cotangent.astype(F32) + grad_norm_in
    return layer, input_grad, (
        grad_inw, grad_outw, d_taps, d_bias, d_shift, d_logs, d_skip, grad_gain, d_gate_gain
    )


def moved(x, step):
    n_rep, n = lax.axis_size("replica"), lax.axis_size("shard")
    perm = []
    for r in range(n_rep):
        for s in range(n):
            to_r, to_s = step(r, s)
            perm.append((r * n + s, to_r * n + to_s))
    return lax.ppermute(x, ("replica", "shard"), perm)


def pick(x, i):
    return lax.dynamic_index_in_dim(x, i, 0, keepdims=False)


def ring_all(x, index, n, step):
    got = jnp.stack([x] + [moved(x, functools.partial(step, k)) for k in range(1, n)])
    return jnp.stack([pick(got, lax.rem(index - j + n, n)) for j in range(n)])


def ring_sum(parts, index, n, step):
    total = pick(parts, index).astype(F32)
    for k in range(1, n):
        total = total + moved(pick(parts, lax.rem(index + k, n)), functools.partial(step, k))
    return total


def shard_step(k, r, s):
    return r, (s + k) % lax.axis_size("shard")


def chip_step(k, r, s):
    return (r + 2 * k) % lax.axis_size("replica"), s


def core_step(r, s):
    return r ^ 1, s


def both_halves(mine, core, axis):
    other = moved(mine, core_step)
    first = jnp.where(core == 0, mine, other)
    second = jnp.where(core == 0, other, mine)
    return jnp.stack([first, second], axis=axis)


def gather_weight(shard, core, me, n):
    half = pick(shard.reshape(2, -1, shard.shape[1]), core)
    mine = ring_all(half, me, n, shard_step)
    return both_halves(mine, core, 1).reshape(-1, shard.shape[1])


def reduce_grad(grad, core, me, n, chip, chips, kind):
    columns = grad.shape[1]
    blocks = grad.astype(kind).reshape(n, 2, -1, columns)
    keep = lax.dynamic_index_in_dim(blocks, core, 1, keepdims=False)
    send = lax.dynamic_index_in_dim(blocks, 1 - core, 1, keepdims=False)
    pair = (keep.astype(F32) + moved(send, core_step).astype(F32)).astype(kind)
    mine = ring_sum(pair, me, n, shard_step).astype(kind)
    piece = ring_sum(mine.reshape(chips, -1, columns), chip, chips, chip_step).astype(kind)
    half = ring_all(piece, chip, chips, chip_step).reshape(-1, columns)
    return both_halves(half, core, 0).reshape(-1, columns).astype(F32)


def on_device(tokens, cotangent, doc_lengths, *shards):
    n, chips = lax.axis_size("shard"), lax.axis_size("replica") // 2
    me, rep = lax.axis_index("shard"), lax.axis_index("replica")
    core, chip = lax.rem(rep, 2), lax.div(rep, 2)
    small = jnp.concatenate([piece.reshape(-1) for piece in shards[2:]])
    small_all = ring_all(small, me, n, shard_step)
    out_full = gather_weight(shards[1], core, me, n)
    in_shard, small_all = lax.optimization_barrier((shards[0], small_all))
    in_full = gather_weight(in_shard, core, me, n)
    smalls, at = [], 0
    for piece in shards[2:]:
        got = small_all[:, at : at + piece.size].astype(F32)
        at += piece.size
        if piece.ndim == 2:
            got = got.reshape(n, *piece.shape).transpose(1, 0, 2).reshape(piece.shape[0], -1)
        else:
            got = got.reshape(-1)
        smalls.append(got)
    gain_vec = smalls[5]
    layer, input_grad, grads = device_part(
        tokens, cotangent, doc_lengths[0], in_full, out_full, (*smalls[:5], smalls[6]), gain_vec
    )
    rows = []
    for piece, grad in zip(shards[2:], grads[2:]):
        if piece.ndim == 2:
            grad = grad.reshape(piece.shape[0], n, -1).transpose(1, 0, 2)
        rows.append(grad.reshape(n, -1))
    packed = jnp.concatenate(rows, axis=1)
    unit = 2 * chips * 8 * LANES
    packed = jnp.pad(packed, ((0, 0), (0, -packed.shape[1] % unit))).reshape(-1, LANES)
    reduce = functools.partial(reduce_grad, core=core, me=me, n=n, chip=chip, chips=chips)
    big_out = reduce(grads[1], kind=BF)
    big_in = reduce(grads[0], kind=BF)
    mine = reduce(packed, kind=F32).reshape(-1)
    outs, at = [], 0
    for piece in shards[2:]:
        outs.append(mine[at : at + piece.size].reshape(piece.shape))
        at += piece.size
    return (layer, input_grad, big_in, big_out, *outs)


def solution(mesh):
    tok = P(("replica", "shard"), None)
    weights = (P("shard", None), P("shard", None), P(None, "shard")) + (P("shard"),) * 6
    return jax.shard_map(
        on_device,
        mesh=mesh,
        in_specs=(tok, tok, tok) + weights,
        out_specs=(tok, tok) + weights,
        check_vma=False,
    )
```
